512 devices in a mesh: img: 32 (over x, y), blk: 16 (over z, core).
Axes of the slice: x: 4, y: 8, z: 8, core: 2. Of those that a mesh axis runs over, the one named last changes fastest.
Arguments:
- images: bfloat16 [128, 28, 1792], P('img'), may hold values from -6 to 6
- filters: bfloat16 [8192, 576], P('blk'), may hold values from -0.5 to 0.5
- phases: float32 [8192], P('blk'), may hold values from -3.140625 to 3.140625
- labels: int32 [25088], P('img'), may hold values from 0 to 149
- weights: float32 [150, 8192], P(None, 'blk'), may hold values from -6 to 6
Outputs:
- new_weights: float32 [150, 8192], P(None, 'blk')
- residual: float32 [150, 25088], P(None, 'img')
The draws below stay inside these ranges and needn't reach their ends.
All inputs are finite; a program needn't handle non-finite values.
Results may differ from the reference program's by a relative error of at most 0.015.
Values may be sent and summed in bfloat16 or wider, within the bound.
No kernel may reach another device: no remote copies, remote signals or barrier semaphores. Data moves between devices by JAX's collectives and lax.ppermute only.
A program may use at most 64 MiB of HBM per device.

```python
import math
import jax
import jax.numpy as jnp
from jax import lax

SIDE = 28
CHAN = 64
FILT = 512
LABELS = 150
ITERS = 2
IMAGES = 128
PIXELS = 25088
FEATURES = 8192


def draw_filters(key, part):
    key_values = jax.random.fold_in(key, 11)
    tap_count = 9 * CHAN
    values = jax.random.normal(key_values, (FEATURES, tap_count), jnp.float32)
    return jnp.clip(values / math.sqrt(tap_count), -0.5, 0.5).astype(jnp.bfloat16)


def set_ends(array, key, smallest, high):
    longest = array.shape.index(max(array.shape))
    spots = []
    for shift in (0, 1):
        where = [jax.random.randint(jax.random.fold_in(key, axis), (), 0, length) for axis, length in enumerate(array.shape)]
        where[longest] = (where[longest] + shift) % array.shape[longest]
        spots.append(tuple(where))
    return array.at[spots[0]].set(smallest).at[spots[1]].set(high)


def levels(own_key, shape, split, low, largest):
    def one(axis_at, shards_of):
        draws = jax.random.uniform(jax.random.fold_in(jax.random.fold_in(own_key, 6), axis_at), (shards_of,), jnp.float32, low / len(split), largest / len(split))
        return jnp.repeat(jnp.exp(draws), shape[axis_at] // shards_of).reshape((-1,) + (1,) * (len(shape) - axis_at - 1))

    gain = one(*split[0])
    for cut in split[1:]:
        gain = gain * one(*cut)
    return gain


def noise(stream_key, dims, scale, reach, shards=(), kind=jnp.bfloat16):
    entries = scale * jax.random.normal(stream_key, dims, jnp.float32)
    if shards:
        entries = entries * levels(stream_key, dims, shards, -0.22, 0.18)
    return jnp.clip(entries, -reach, reach).astype(kind)


def setup_inputs(seed: int = 0) -> dict:
    streams_of = jax.random.split(jax.random.key(seed), 6)
    return {
        "images": noise(streams_of[0], (IMAGES, SIDE, SIDE * CHAN), 1.0, 6.0, ((0, 32),)),
        "filters": draw_filters(jax.random.fold_in(streams_of[5], 71), 0),
        "phases": jnp.clip(jax.random.uniform(streams_of[2], (FEATURES,), jnp.float32, -3.140625, 3.140625), -3.140625, 3.140625),
        "labels": set_ends(jax.random.randint(streams_of[3], (PIXELS,), 0, LABELS), jax.random.fold_in(streams_of[3], 1), 0, LABELS - 1).astype(jnp.int32),
        "weights": noise(streams_of[4], (LABELS, FEATURES), 1.0, 6.0, ((1, 16),), jnp.float32),
    }


RIDGE = 0.5
DAMPING = 0.75

def block_features(images, filter_rows, phase_rows):
    count_images = images.shape[0]
    pictures = images.reshape(count_images, SIDE, SIDE, CHAN)
    kernel = filter_rows.reshape(filter_rows.shape[0], 3, 3, CHAN)
    response = lax.conv_general_dilated(pictures, kernel, (2, 2), ((1, 1), (1, 1)), dimension_numbers=('NHWC', 'OHWI', 'CNHW'), preferred_element_type=jnp.float32)
    response = response.reshape(filter_rows.shape[0], count_images * (SIDE // 2) ** 2)
    return (math.sqrt(2.0) * jnp.cos(response + phase_rows[:, None])).astype(jnp.bfloat16)

def solve_with(factor, projected):
    middle = lax.linalg.triangular_solve(factor, projected, left_side=False, lower=True, transpose_a=True)
    return lax.linalg.triangular_solve(factor, middle, left_side=False, lower=True, transpose_a=False)

def reference(images, filters, phases, labels, weights):
    blocks = filters.shape[0] // FILT
    features_all = FILT * blocks
    shrink = 1.0 / math.sqrt(features_all)
    expand = math.sqrt(features_all)
    pixels = labels.shape[0]
    targets = (labels[None, :] == jnp.arange(LABELS, dtype=jnp.int32)[:, None]).astype(jnp.float32)
    filter_blocks = filters.reshape(blocks, FILT, filters.shape[1])
    phase_blocks = phases.reshape(blocks, FILT)
    weight_blocks = weights.reshape(LABELS, blocks, FILT).transpose(1, 0, 2)
    identity = jnp.eye(FILT, dtype=jnp.float32)

    def first_pass(summed, inputs):
        filter_rows, phase_rows, weight_now = inputs
        features = block_features(images, filter_rows, phase_rows)
        gram = lax.dot_general(features.astype(jnp.float32), features.astype(jnp.float32), (((1,), (1,)), ((), ())), preferred_element_type=jnp.float32) + RIDGE * pixels * identity
        factor = jnp.linalg.cholesky(gram)
        partial_value = (shrink * jnp.dot(weight_now.astype(jnp.bfloat16).astype(jnp.float32), features.astype(jnp.float32), preferred_element_type=jnp.float32)).astype(jnp.bfloat16)
        return (summed + partial_value, factor)
    zeros_start = jnp.zeros((LABELS, pixels), jnp.float32)
    predicted, factors = lax.scan(first_pass, zeros_start, (filter_blocks, phase_blocks, weight_blocks))
    residual = targets - predicted
    for step in range(ITERS):
        residual_half = residual.astype(jnp.bfloat16)

        def update_pass(summed, inputs):
            filter_rows, phase_rows, weight_now, factor = inputs
            features = block_features(images, filter_rows, phase_rows)
            projected = lax.dot_general(residual_half.astype(jnp.float32), features.astype(jnp.float32), (((1,), (1,)), ((), ())), preferred_element_type=jnp.float32)
            change = expand * solve_with(factor, projected)
            weight_next = weight_now + DAMPING * change
            partial_value = (shrink * jnp.dot(weight_next.astype(jnp.bfloat16).astype(jnp.float32), features.astype(jnp.float32), preferred_element_type=jnp.float32)).astype(jnp.bfloat16)
            return (summed + partial_value, weight_next)
        predicted, weight_blocks = lax.scan(update_pass, zeros_start, (filter_blocks, phase_blocks, weight_blocks, factors))
        residual = targets - predicted
    new_weights = weight_blocks.transpose(1, 0, 2).reshape(LABELS, features_all)
    return (new_weights, residual)
```

```python
import math

import jax
import jax.numpy as jnp
import numpy as np
from jax import lax
from jax.experimental import pallas as pl
from jax.experimental.pallas import tpu as pltpu
from jax.sharding import PartitionSpec as P

SIDE = 28
CHAN = 64
FILT = 512
LABELS = 150
ITERS = 2
RIDGE = 0.5
DAMPING = 0.75

OUT = SIDE // 2
PAIR = 2 * CHAN
DEEP = 6 * PAIR
ROWS = 160
TILE = 128
BF16 = jnp.bfloat16
F32 = jnp.float32


def cosine_coefficients(degree):
    nodes = np.cos((np.arange(200) + 0.5) * math.pi / 200)
    squares = (nodes + 1) * 0.5 * math.pi**2
    fit = np.polynomial.Chebyshev.fit(
        squares, math.sqrt(2.0) * np.cos(np.sqrt(squares)), degree, domain=[0, math.pi**2]
    )
    return [float(c) for c in fit.convert(kind=np.polynomial.Polynomial).coef]


COS = cosine_coefficients(7)


def scaled_cosine(x):
    turns = jnp.floor(x * (0.5 / math.pi) + 0.5)
    y = (x - turns * 6.28125) - turns * (2 * math.pi - 6.28125)
    u = y * y
    value = u * COS[-1] + COS[-2]
    for c in COS[-3::-1]:
        value = value * u + c
    return value


def up8(n):
    return -(-n // 8) * 8


def call(kernel, outs, *args, scratch=(), name=None, flops=0):
    specs = [
        pl.BlockSpec(memory_space=pltpu.SMEM if a.dtype == jnp.int32 and a.ndim == 1 else pltpu.VMEM)
        for a in args
    ]
    size = sum(math.prod(a.shape) * a.dtype.itemsize for a in (*args, *outs))
    return pl.pallas_call(
        kernel,
        out_shape=outs,
        in_specs=specs,
        out_specs=[pl.BlockSpec(memory_space=pltpu.VMEM)] * len(outs),
        scratch_shapes=scratch,
        name=name,
        cost_estimate=pl.CostEstimate(flops=flops, bytes_accessed=size, transcendentals=0),
    )(*args)


def contract_last(a, b):
    return lax.dot_general(a, b, (((1,), (1,)), ((), ())), preferred_element_type=F32)


def store_prediction(stack_ref, weights, features, shrink):
    for t in range(features.shape[1] // TILE):
        part = jnp.dot(weights, features[:, t * TILE : (t + 1) * TILE], preferred_element_type=F32)
        stack_ref[t * ROWS : (t + 1) * ROWS] = (part * shrink).astype(BF16)
    used = features.shape[1] // TILE * ROWS
    if used < stack_ref.shape[0]:
        stack_ref[used:] = jnp.zeros((stack_ref.shape[0] - used, TILE), BF16)


def feature_kernel(img, filt, phase, feat, gram, rows32, patches, taps):
    sides, count = img.shape[:2]
    per = OUT * OUT
    patches[...] = jnp.zeros_like(patches)
    for c in range(OUT):
        for row in range(sides):
            rows32[row * count : (row + 1) * count] = img[row, :, c * PAIR : (c + 1) * PAIR].astype(F32)
        for n in range(count):
            even = rows32[pl.ds(n, OUT, stride=2 * count), :]
            odd = rows32[pl.ds(count + n, OUT, stride=2 * count), :]
            for side in range(2):
                at = c + 1 - side
                if at >= OUT:
                    continue
                first = n * per + at
                patches[2 + side, pl.ds(first, OUT, stride=OUT), :] = even
                patches[4 + side, pl.ds(first, OUT, stride=OUT), :] = odd
                patches[side, pl.ds(first + OUT, OUT - 1, stride=OUT), :] = odd[: OUT - 1]
    windows = jnp.concatenate([patches[k].astype(BF16) for k in range(DEEP // PAIR)], axis=1)
    third = DEEP // 3
    for k in range(3):
        taps[k * third : k * third + CHAN] = jnp.zeros((CHAN, FILT), BF16)
        taps[k * third + CHAN : (k + 1) * third] = filt[k * 3 * CHAN : (k + 1) * 3 * CHAN]
    for block in range(FILT // TILE):
        rows = slice(block * TILE, (block + 1) * TILE)
        response = lax.dot_general(
            taps[:, rows], windows, (((0,), (1,)), ((), ())), preferred_element_type=F32
        )
        turned = jnp.broadcast_to(phase[:, rows], (TILE, TILE)).T
        values = scaled_cosine(response + turned[:, :1])
        live = lax.broadcasted_iota(jnp.int32, values.shape, 1) < count * per
        feat[rows] = jnp.where(live, values, 0.0).astype(BF16)
    at = 0
    for i in range(FILT // TILE):
        for j in range(i + 1):
            gram[at : at + TILE] = contract_last(
                feat[i * TILE : (i + 1) * TILE], feat[j * TILE : (j + 1) * TILE]
            )
            at += TILE


def first_predict_kernel(shrink, weights, feat, stack, wide):
    wide[...] = jnp.zeros_like(wide)
    wide[:LABELS] = weights[...]
    store_prediction(stack, wide[...].astype(BF16), feat[...], shrink)


def summed(ref, parts):
    rows = ref.shape[0] // parts
    total = ref[:rows].astype(F32)
    for k in range(1, parts):
        total += ref[k * rows : (k + 1) * rows].astype(F32)
    return total


def copies(ref, value, parts):
    rows = value.shape[0]
    for k in range(parts):
        ref[k * rows : (k + 1) * rows] = value


def residual_kernel(parts, place, got, labels, out):
    total = summed(got, parts)
    rows = total.shape[0]
    line = lax.broadcasted_iota(jnp.int32, total.shape, 0) + place[0] * rows
    targets = jnp.zeros_like(total)
    for t in range(labels.shape[0]):
        targets += jnp.where(line - t * ROWS == labels[t : t + 1], 1.0, 0.0)
    copies(out, (targets - total).astype(BF16), parts)


def gram_kernel(parts, got, out):
    copies(out, summed(got, parts), parts)


def unstacked(ref, tiles):
    return jnp.concatenate([ref[t * ROWS : (t + 1) * ROWS] for t in range(tiles)], axis=1)


def project_kernel(parts, got, feat, out, spread):
    tiles = feat.shape[1] // TILE
    projected = contract_last(unstacked(got, tiles), feat[...])
    own = ROWS // parts
    rows = spread.shape[0] // parts
    lanes = FILT // TILE
    if own * lanes < rows:
        spread[...] = jnp.zeros_like(spread)
    for k in range(own):
        for t in range(lanes):
            spread[pl.ds(k * lanes + t, parts, stride=rows), :] = projected[
                k * parts : (k + 1) * parts, t * TILE : (t + 1) * TILE
            ]
    out[...] = spread[...].astype(out.dtype)


def two_halves(x):
    high = x.astype(BF16)
    return high, (x - high.astype(F32)).astype(BF16)


def inverse_kernel(ridge, got, matrix, inverse, left, value):
    at = 0
    for i in range(FILT // TILE):
        for j in range(i + 1):
            part = got[at : at + TILE]
            at += TILE
            if i == j:
                eye = lax.broadcasted_iota(jnp.int32, part.shape, 0) == lax.broadcasted_iota(jnp.int32, part.shape, 1)
                part = part + jnp.where(eye, ridge, 0.0)
            else:
                value[j * TILE : (j + 1) * TILE, i * TILE : (i + 1) * TILE] = part.T
            value[i * TILE : (i + 1) * TILE, j * TILE : (j + 1) * TILE] = part
    h = value[...]
    high, rest = two_halves(h)
    matrix[:FILT] = high
    matrix[FILT:] = rest
    left[:, :FILT] = high
    left[:, FILT : 2 * FILT] = high
    left[:, 2 * FILT :] = rest
    largest = jnp.max(jnp.sum(jnp.abs(h), axis=0, keepdims=True))
    scale = 1.0 / largest
    low = 0.98 * ridge * scale
    eye = lax.broadcasted_iota(jnp.int32, h.shape, 0) == lax.broadcasted_iota(jnp.int32, h.shape, 1)
    gain = 4.0 / ((1.0 + low) * (1.0 + low))
    value[...] = gain * scale * (jnp.where(eye, 1.0 + low, 0.0) - scale * h)

    def more(low):
        return low < 1.0 - 1e-4

    def step(low):
        gain = 4.0 / ((1.0 + low) * (1.0 + low))
        x = value[...]
        xh, xl = two_halves(x)
        y = jnp.dot(left[...], jnp.concatenate([xh, xl, xh], axis=0), preferred_element_type=F32)
        yh, yl = two_halves(y)
        xy = jnp.dot(
            jnp.concatenate([xh, xh, xl], axis=1),
            jnp.concatenate([yh, yl, yh], axis=0),
            preferred_element_type=F32,
        )
        value[...] = gain * ((1.0 + low) * x - xy)
        return jnp.minimum(gain * low, 1.0)

    lax.while_loop(more, step, gain * low)
    high, rest = two_halves(value[...])
    inverse[:FILT] = high
    inverse[FILT:] = rest


def times(x, halves):
    rows = x.shape[0]
    both = jnp.concatenate([x.astype(BF16).astype(F32), x - x.astype(BF16).astype(F32)], axis=0).astype(BF16)
    found = jnp.dot(both, halves[:FILT], preferred_element_type=F32) + jnp.dot(
        both, halves[FILT:], preferred_element_type=F32
    )
    return found[:rows] + found[rows:]


def solve_kernel(parts, factor, place, got, weights, matrix, inverse, own_out, out, folded, wide):
    own = ROWS // parts
    lanes = FILT // TILE
    rows = got.shape[0] // parts
    tall = folded.shape[0] // lanes
    folded[...] = jnp.zeros_like(folded)
    folded[:rows] = summed(got, parts)
    projected = jnp.concatenate([folded[pl.ds(t, tall, stride=lanes), :] for t in range(lanes)], axis=1)
    change = times(projected, inverse)
    for _ in range(2):
        change += times(projected - times(change, matrix), inverse)
    if weights.shape[0] == tall:
        now = weights[...]
    else:
        wide[...] = jnp.zeros_like(wide)
        wide[:LABELS] = weights[...]
        held = [wide[pl.ds(place[0] + k * parts, 1), :] for k in range(own)]
        if own < tall:
            held.append(jnp.zeros((tall - own, FILT), F32))
        now = jnp.concatenate(held, axis=0)
    new = now + factor * change
    own_out[...] = new
    for t in range(lanes):
        folded[pl.ds(t, tall, stride=lanes), :] = new[:, t * TILE : (t + 1) * TILE]
    copies(out, folded[:rows].astype(out.dtype), parts)


def predict_kernel(parts, shrink, keep, got, feat, *refs):
    stack = refs[0]
    spread = refs[-1]
    own = ROWS // parts
    rows = got.shape[0] // parts
    lanes = FILT // TILE
    spread[...] = got[...].astype(F32)
    weights = jnp.concatenate(
        [
            jnp.concatenate(
                [spread[pl.ds(k * lanes + t, parts, stride=rows), :] for t in range(lanes)], axis=1
            )
            for k in range(own)
        ],
        axis=0,
    )
    if keep:
        refs[1][...] = weights[:LABELS]
    store_prediction(stack, weights.astype(BF16), feat[...], shrink)


def output_kernel(got, out):
    tiles = -(-out.shape[1] // TILE)
    for t in range(tiles):
        wide = min(TILE, out.shape[1] - t * TILE)
        out[:, t * TILE : t * TILE + wide] = got[t * ROWS : t * ROWS + LABELS, :wide].astype(F32)


def exchange(x, axis):
    parts = lax.axis_size(axis)
    pieces = x.reshape(parts, x.shape[0] // parts, x.shape[1])
    return lax.all_to_all(pieces, axis, 0, 0, tiled=True).reshape(x.shape)


def shards(images, filters, phases, labels, weights):
    groups, blocks = lax.axis_size("img"), lax.axis_size("blk")
    here = labels.shape[0]
    ridge = RIDGE * here * groups
    shrink = 1.0 / math.sqrt(FILT * blocks)
    factor = DAMPING * math.sqrt(FILT * blocks)
    lane_tiles = -(-here // TILE)
    padded = lane_tiles * TILE
    stack_rows = up8(-(-lane_tiles * ROWS // blocks)) * blocks
    fold_rows = up8(ROWS // groups * (FILT // TILE)) * groups
    gram_rows = (FILT // TILE) * (FILT // TILE + 1) // 2 * TILE
    tall = up8(ROWS // groups)

    img_place = lax.axis_index("img").astype(jnp.int32).reshape(1)
    blk_place = lax.axis_index("blk").astype(jnp.int32).reshape(1)
    label_tiles = jnp.pad(labels, (0, padded - here), constant_values=-100000).reshape(lane_tiles, TILE)

    def shape(*dims, dtype=F32):
        return jax.ShapeDtypeStruct(dims, dtype)

    feat, gram_part = call(
        feature_kernel, [shape(FILT, padded, dtype=BF16), shape(gram_rows, TILE)],
        images.transpose(1, 0, 2), filters.T, phases.reshape(1, FILT),
        scratch=[
            pltpu.VMEM((SIDE * images.shape[0], PAIR), F32),
            pltpu.VMEM((DEEP // PAIR, padded, PAIR), F32),
            pltpu.VMEM((DEEP, FILT), BF16),
        ],
        name="features", flops=2 * 10**9,
    )
    (stack,) = call(
        lambda *r: first_predict_kernel(shrink, *r), [shape(stack_rows, TILE, dtype=BF16)], weights, feat,
        scratch=[pltpu.VMEM((ROWS, FILT), F32)], name="predict", flops=10**8,
    )

    def residual_of(stack):
        (mine,) = call(
            lambda *r: residual_kernel(blocks, *r), [shape(stack_rows, TILE, dtype=BF16)],
            blk_place, exchange(stack, "blk"), label_tiles, name="residual",
        )
        return exchange(mine, "blk")

    def projection_of(residual):
        (parts,) = call(
            lambda *r: project_kernel(groups, *r), [shape(fold_rows, TILE)],
            residual, feat, scratch=[pltpu.VMEM((fold_rows, TILE), F32)], name="project", flops=10**8,
        )
        return exchange(parts, "img")

    residual = residual_of(stack)
    (gram_sum,) = call(
        lambda *r: gram_kernel(groups, *r), [shape(gram_rows, TILE)], exchange(gram_part, "img"), name="gram",
    )
    matrix, inverse = call(
        lambda *r: inverse_kernel(ridge, *r), [shape(2 * FILT, FILT, dtype=BF16)] * 2,
        exchange(gram_sum, "img"),
        scratch=[pltpu.VMEM((FILT, 3 * FILT), BF16), pltpu.VMEM((FILT, FILT), F32)],
        name="inverse", flops=14 * 10**9,
    )
    own = weights
    for step in range(ITERS):
        last = step == ITERS - 1
        kind = F32 if last else BF16
        projected = projection_of(residual)
        own, spread = call(
            lambda *r: solve_kernel(groups, factor, *r), [shape(tall, FILT), shape(fold_rows, TILE, dtype=kind)],
            img_place, projected, own, matrix, inverse,
            scratch=[pltpu.VMEM((tall * (FILT // TILE), TILE), F32), pltpu.VMEM((ROWS, FILT), F32)],
            name="solve", flops=10**8,
        )
        found = call(
            lambda *r: predict_kernel(groups, shrink, last, *r),
            [shape(stack_rows, TILE, dtype=BF16)] + ([shape(LABELS, FILT)] if last else []),
            exchange(spread, "img"), feat,
            scratch=[pltpu.VMEM((fold_rows, TILE), F32)], name="predict", flops=10**8,
        )
        residual = residual_of(found[0])
    (out,) = call(output_kernel, [shape(LABELS, here)], residual, name="output")
    return (found[1], out)


def solution(mesh):
    return jax.shard_map(
        shards,
        mesh=mesh,
        in_specs=(P("img", None, None), P("blk", None), P("blk"), P("img"), P(None, "blk")),
        out_specs=(P(None, "blk"), P(None, "img")),
        check_vma=False,
    )
```

```python
import math

import jax
import jax.numpy as jnp
import numpy as np
from jax import lax
from jax.experimental import pallas as pl
from jax.experimental.pallas import tpu as pltpu
from jax.sharding import PartitionSpec as P

SIDE = 28
CHAN = 64
FILT = 512
LABELS = 150
ITERS = 2
RIDGE = 0.5
DAMPING = 0.75

OUT = SIDE // 2
PAIR = 2 * CHAN
DEEP = 6 * PAIR
ROWS = 160
TILE = 128
BF16 = jnp.bfloat16
F32 = jnp.float32


def cosine_coefficients(degree):
    nodes = np.cos((np.arange(200) + 0.5) * math.pi / 200)
    squares = (nodes + 1) * 0.5 * math.pi**2
    fit = np.polynomial.Chebyshev.fit(
        squares, math.sqrt(2.0) * np.cos(np.sqrt(squares)), degree, domain=[0, math.pi**2]
    )
    return [float(c) for c in fit.convert(kind=np.polynomial.Polynomial).coef]


COS = cosine_coefficients(7)


def scaled_cosine(x):
    turns = jnp.floor(x * (0.5 / math.pi) + 0.5)
    y = (x - turns * 6.28125) - turns * (2 * math.pi - 6.28125)
    u = y * y
    value = u * COS[-1] + COS[-2]
    for c in COS[-3::-1]:
        value = value * u + c
    return value


def up8(n):
    return -(-n // 8) * 8


def call(kernel, outs, *args, scratch=(), name=None, flops=0):
    specs = [
        pl.BlockSpec(memory_space=pltpu.SMEM if a.dtype == jnp.int32 and a.ndim == 1 else pltpu.VMEM)
        for a in args
    ]
    size = sum(math.prod(a.shape) * a.dtype.itemsize for a in (*args, *outs))
    return pl.pallas_call(
        kernel,
        out_shape=outs,
        in_specs=specs,
        out_specs=[pl.BlockSpec(memory_space=pltpu.VMEM)] * len(outs),
        scratch_shapes=scratch,
        compiler_params=pltpu.CompilerParams(vmem_limit_bytes=20 * 2**20),
        name=name,
        cost_estimate=pl.CostEstimate(flops=flops, bytes_accessed=size, transcendentals=0),
    )(*args)


def contract_last(a, b):
    return lax.dot_general(a, b, (((1,), (1,)), ((), ())), preferred_element_type=F32)


def store_prediction(stack_ref, weights, features, shrink):
    for t in range(features.shape[1] // TILE):
        part = jnp.dot(weights, features[:, t * TILE : (t + 1) * TILE], preferred_element_type=F32)
        stack_ref[t * ROWS : (t + 1) * ROWS] = (part * shrink).astype(BF16)
    used = features.shape[1] // TILE * ROWS
    if used < stack_ref.shape[0]:
        stack_ref[used:] = jnp.zeros((stack_ref.shape[0] - used, TILE), BF16)


def feature_kernel(img, filt, phase, feat, gram, rows32, patches, taps):
    sides, count = img.shape[:2]
    per = OUT * OUT
    patches[...] = jnp.zeros_like(patches)
    for c in range(OUT):
        for row in range(sides):
            rows32[row * count : (row + 1) * count] = img[row, :, c * PAIR : (c + 1) * PAIR].astype(F32)
        for n in range(count):
            even = rows32[pl.ds(n, OUT, stride=2 * count), :]
            odd = rows32[pl.ds(count + n, OUT, stride=2 * count), :]
            for side in range(2):
                at = c + 1 - side
                if at >= OUT:
                    continue
                first = n * per + at
                patches[2 + side, pl.ds(first, OUT, stride=OUT), :] = even
                patches[4 + side, pl.ds(first, OUT, stride=OUT), :] = odd
                patches[side, pl.ds(first + OUT, OUT - 1, stride=OUT), :] = odd[: OUT - 1]
    windows = jnp.concatenate([patches[k].astype(BF16) for k in range(DEEP // PAIR)], axis=1)
    third = DEEP // 3
    for k in range(3):
        taps[k * third : k * third + CHAN] = jnp.zeros((CHAN, FILT), BF16)
        taps[k * third + CHAN : (k + 1) * third] = filt[k * 3 * CHAN : (k + 1) * 3 * CHAN]
    for block in range(FILT // TILE):
        rows = slice(block * TILE, (block + 1) * TILE)
        response = lax.dot_general(
            taps[:, rows], windows, (((0,), (1,)), ((), ())), preferred_element_type=F32
        )
        turned = jnp.broadcast_to(phase[:, rows], (TILE, TILE)).T
        values = scaled_cosine(response + turned[:, :1])
        live = lax.broadcasted_iota(jnp.int32, values.shape, 1) < count * per
        feat[rows] = jnp.where(live, values, 0.0).astype(BF16)
    at = 0
    for i in range(FILT // TILE):
        for j in range(i + 1):
            gram[at : at + TILE] = contract_last(
                feat[i * TILE : (i + 1) * TILE], feat[j * TILE : (j + 1) * TILE]
            )
            at += TILE


def first_predict_kernel(shrink, weights, feat, stack, wide):
    wide[...] = jnp.zeros_like(wide)
    wide[:LABELS] = weights[...]
    store_prediction(stack, wide[...].astype(BF16), feat[...], shrink)


def summed(ref, parts):
    rows = ref.shape[0] // parts
    total = ref[:rows].astype(F32)
    for k in range(1, parts):
        total += ref[k * rows : (k + 1) * rows].astype(F32)
    return total


def copies(ref, value, parts):
    rows = value.shape[0]
    for k in range(parts):
        ref[k * rows : (k + 1) * rows] = value


def residual_kernel(parts, place, got, labels, out):
    total = summed(got, parts)
    rows = total.shape[0]
    line = lax.broadcasted_iota(jnp.int32, total.shape, 0) + place[0] * rows
    targets = jnp.zeros_like(total)
    for t in range(labels.shape[0]):
        targets += jnp.where(line - t * ROWS == labels[t : t + 1], 1.0, 0.0)
    out[...] = (targets - total).astype(BF16)


def gram_kernel(parts, got, out):
    copies(out, summed(got, parts), parts)


def unstacked(ref, tiles):
    return jnp.concatenate([ref[t * ROWS : (t + 1) * ROWS] for t in range(tiles)], axis=1)


def project_kernel(parts, got, feat, out, spread):
    tiles = feat.shape[1] // TILE
    projected = contract_last(unstacked(got, tiles), feat[...])
    own = ROWS // parts
    rows = spread.shape[0] // parts
    lanes = FILT // TILE
    if own * lanes < rows:
        spread[...] = jnp.zeros_like(spread)
    for k in range(own):
        for t in range(lanes):
            spread[pl.ds(k * lanes + t, parts, stride=rows), :] = projected[
                k * parts : (k + 1) * parts, t * TILE : (t + 1) * TILE
            ]
    out[...] = spread[...].astype(out.dtype)


def two_halves(x):
    high = x.astype(BF16)
    return high, (x - high.astype(F32)).astype(BF16)


def inverse_kernel(ridge, got, matrix, inverse, left, value):
    at = 0
    for i in range(FILT // TILE):
        for j in range(i + 1):
            part = got[at : at + TILE]
            at += TILE
            if i == j:
                eye = lax.broadcasted_iota(jnp.int32, part.shape, 0) == lax.broadcasted_iota(jnp.int32, part.shape, 1)
                part = part + jnp.where(eye, ridge, 0.0)
            else:
                value[j * TILE : (j + 1) * TILE, i * TILE : (i + 1) * TILE] = part.T
            value[i * TILE : (i + 1) * TILE, j * TILE : (j + 1) * TILE] = part
    h = value[...]
    high, rest = two_halves(h)
    matrix[:FILT] = high
    matrix[FILT:] = rest
    left[:, :FILT] = high
    left[:, FILT : 2 * FILT] = high
    left[:, 2 * FILT :] = rest
    largest = jnp.max(jnp.sum(jnp.abs(h), axis=0, keepdims=True))
    scale = 1.0 / largest
    low = 0.98 * ridge * scale
    eye = lax.broadcasted_iota(jnp.int32, h.shape, 0) == lax.broadcasted_iota(jnp.int32, h.shape, 1)
    gain = 4.0 / ((1.0 + low) * (1.0 + low))
    value[...] = gain * scale * (jnp.where(eye, 1.0 + low, 0.0) - scale * h)

    def more(low):
        return low < 1.0 - 1e-4

    def step(low):
        gain = 4.0 / ((1.0 + low) * (1.0 + low))
        x = value[...]
        xh, xl = two_halves(x)
        y = jnp.dot(left[...], jnp.concatenate([xh, xl, xh], axis=0), preferred_element_type=F32)
        yh, yl = two_halves(y)
        xy = jnp.dot(
            jnp.concatenate([xh, xh, xl], axis=1),
            jnp.concatenate([yh, yl, yh], axis=0),
            preferred_element_type=F32,
        )
        value[...] = gain * ((1.0 + low) * x - xy)
        return jnp.minimum(gain * low, 1.0)

    lax.while_loop(more, step, gain * low)
    high, rest = two_halves(value[...])
    inverse[:FILT] = high
    inverse[FILT:] = rest


def times(x, halves):
    rows = x.shape[0]
    both = jnp.concatenate([x.astype(BF16).astype(F32), x - x.astype(BF16).astype(F32)], axis=0).astype(BF16)
    found = jnp.dot(both, halves[:FILT], preferred_element_type=F32) + jnp.dot(
        both, halves[FILT:], preferred_element_type=F32
    )
    return found[:rows] + found[rows:]


def solve_kernel(parts, factor, place, got, weights, matrix, inverse, own_out, out, folded, wide):
    own = ROWS // parts
    lanes = FILT // TILE
    rows = got.shape[0] // parts
    tall = folded.shape[0] // lanes
    folded[...] = jnp.zeros_like(folded)
    folded[:rows] = summed(got, parts)
    projected = jnp.concatenate([folded[pl.ds(t, tall, stride=lanes), :] for t in range(lanes)], axis=1)
    change = times(projected, inverse)
    for _ in range(2):
        change += times(projected - times(change, matrix), inverse)
    if weights.shape[0] == tall:
        now = weights[...]
    else:
        wide[...] = jnp.zeros_like(wide)
        wide[:LABELS] = weights[...]
        held = [wide[pl.ds(place[0] + k * parts, 1), :] for k in range(own)]
        if own < tall:
            held.append(jnp.zeros((tall - own, FILT), F32))
        now = jnp.concatenate(held, axis=0)
    new = now + factor * change
    own_out[...] = new
    for t in range(lanes):
        folded[pl.ds(t, tall, stride=lanes), :] = new[:, t * TILE : (t + 1) * TILE]
    copies(out, folded[:rows].astype(out.dtype), parts)


def predict_kernel(parts, shrink, keep, got, feat, *refs):
    stack = refs[0]
    spread = refs[-1]
    own = ROWS // parts
    rows = got.shape[0] // parts
    lanes = FILT // TILE
    spread[...] = got[...].astype(F32)
    weights = jnp.concatenate(
        [
            jnp.concatenate(
                [spread[pl.ds(k * lanes + t, parts, stride=rows), :] for t in range(lanes)], axis=1
            )
            for k in range(own)
        ],
        axis=0,
    )
    if keep:
        refs[1][...] = weights[:LABELS]
    store_prediction(stack, weights.astype(BF16), feat[...], shrink)


def output_kernel(got, out):
    tiles = -(-out.shape[1] // TILE)
    for t in range(tiles):
        wide = min(TILE, out.shape[1] - t * TILE)
        out[:, t * TILE : t * TILE + wide] = got[t * ROWS : t * ROWS + LABELS, :wide].astype(F32)


def exchange(x, axis):
    parts = lax.axis_size(axis)
    pieces = x.reshape(parts, x.shape[0] // parts, x.shape[1])
    return lax.all_to_all(pieces, axis, 0, 0, tiled=True).reshape(x.shape)


def shards(images, filters, phases, labels, weights):
    groups, blocks = lax.axis_size("img"), lax.axis_size("blk")
    here = labels.shape[0]
    ridge = RIDGE * here * groups
    shrink = 1.0 / math.sqrt(FILT * blocks)
    factor = DAMPING * math.sqrt(FILT * blocks)
    lane_tiles = -(-here // TILE)
    padded = lane_tiles * TILE
    stack_rows = up8(-(-lane_tiles * ROWS // blocks)) * blocks
    fold_rows = up8(ROWS // groups * (FILT // TILE)) * groups
    gram_rows = (FILT // TILE) * (FILT // TILE + 1) // 2 * TILE
    tall = up8(ROWS // groups)

    img_place = lax.axis_index("img").astype(jnp.int32).reshape(1)
    blk_place = lax.axis_index("blk").astype(jnp.int32).reshape(1)
    label_tiles = jnp.pad(labels, (0, padded - here), constant_values=-100000).reshape(lane_tiles, TILE)

    def shape(*dims, dtype=F32):
        return jax.ShapeDtypeStruct(dims, dtype)

    feat, gram_part = call(
        feature_kernel, [shape(FILT, padded, dtype=BF16), shape(gram_rows, TILE)],
        images.transpose(1, 0, 2), filters.T, phases.reshape(1, FILT),
        scratch=[
            pltpu.VMEM((SIDE * images.shape[0], PAIR), F32),
            pltpu.VMEM((DEEP // PAIR, padded, PAIR), F32),
            pltpu.VMEM((DEEP, FILT), BF16),
        ],
        name="features", flops=2 * 10**9,
    )
    (stack,) = call(
        lambda *r: first_predict_kernel(shrink, *r), [shape(stack_rows, TILE, dtype=BF16)], weights, feat,
        scratch=[pltpu.VMEM((ROWS, FILT), F32)], name="predict", flops=10**8,
    )

    def residual_of(stack):
        (mine,) = call(
            lambda *r: residual_kernel(blocks, *r), [shape(stack_rows // blocks, TILE, dtype=BF16)],
            blk_place, exchange(stack, "blk"), label_tiles, name="residual",
        )
        return lax.all_gather(mine, "blk", tiled=True)

    def projection_of(residual):
        (parts,) = call(
            lambda *r: project_kernel(groups, *r), [shape(fold_rows, TILE)],
            residual, feat, scratch=[pltpu.VMEM((fold_rows, TILE), F32)], name="project", flops=10**8,
        )
        return exchange(parts, "img")

    residual = residual_of(stack)
    (gram_sum,) = call(
        lambda *r: gram_kernel(groups, *r), [shape(gram_rows, TILE)], exchange(gram_part, "img"), name="gram",
    )
    matrix, inverse = call(
        lambda *r: inverse_kernel(ridge, *r), [shape(2 * FILT, FILT, dtype=BF16)] * 2,
        exchange(gram_sum, "img"),
        scratch=[pltpu.VMEM((FILT, 3 * FILT), BF16), pltpu.VMEM((FILT, FILT), F32)],
        name="inverse", flops=14 * 10**9,
    )
    own = weights
    for step in range(ITERS):
        last = step == ITERS - 1
        projected = projection_of(residual)
        own, spread = call(
            lambda *r: solve_kernel(groups, factor, *r), [shape(tall, FILT), shape(fold_rows, TILE, dtype=BF16)],
            img_place, projected, own, matrix, inverse,
            scratch=[pltpu.VMEM((tall * (FILT // TILE), TILE), F32), pltpu.VMEM((ROWS, FILT), F32)],
            name="solve", flops=10**8,
        )
        found = call(
            lambda *r: predict_kernel(groups, shrink, last, *r),
            [shape(stack_rows, TILE, dtype=BF16)] + ([shape(LABELS, FILT)] if last else []),
            exchange(spread, "img"), feat,
            scratch=[pltpu.VMEM((fold_rows, TILE), F32)], name="predict", flops=10**8,
        )
        residual = residual_of(found[0])
    (out,) = call(output_kernel, [shape(LABELS, here)], residual, name="output")
    return (found[1], out)


def solution(mesh):
    return jax.shard_map(
        shards,
        mesh=mesh,
        in_specs=(P("img", None, None), P("blk", None), P("blk"), P("img"), P(None, "blk")),
        out_specs=(P(None, "blk"), P(None, "img")),
        check_vma=False,
    )
```

```python
import math

import jax
import jax.numpy as jnp
import numpy as np
from jax import lax
from jax.experimental import pallas as pl
from jax.experimental.pallas import tpu as pltpu
from jax.sharding import PartitionSpec as P


SIDE = 28
CHAN = 64
FILT = 512
LABELS = 150
ITERS = 2
RIDGE = 0.5
DAMPING = 0.75

OUT = SIDE // 2
PAIR = 2 * CHAN
DEEP = 6 * PAIR
ROWS = 160
TILE = 128
BF16 = jnp.bfloat16
F32 = jnp.float32


def cosine_coefficients(degree):
    nodes = np.cos((np.arange(200) + 0.5) * math.pi / 200)
    squares = (nodes + 1) * 0.5 * math.pi**2
    fit = np.polynomial.Chebyshev.fit(
        squares, math.sqrt(2.0) * np.cos(np.sqrt(squares)), degree, domain=[0, math.pi**2]
    )
    return [float(c) for c in fit.convert(kind=np.polynomial.Polynomial).coef]


COS = cosine_coefficients(7)


def scaled_cosine(x):
    turns = jnp.floor(x * (0.5 / math.pi) + 0.5)
    y = (x - turns * 6.28125) - turns * (2 * math.pi - 6.28125)
    u = y * y
    value = u * COS[-1] + COS[-2]
    for c in COS[-3::-1]:
        value = value * u + c
    return value


def up8(n):
    return -(-n // 8) * 8


def call(kernel, outs, *args, scratch=(), flops=0):
    specs = [
        pl.BlockSpec(memory_space=pltpu.SMEM if a.dtype == jnp.int32 and a.ndim == 1 else pltpu.VMEM)
        for a in args
    ]
    size = sum(math.prod(a.shape) * a.dtype.itemsize for a in (*args, *outs))
    return pl.pallas_call(
        kernel,
        out_shape=outs,
        in_specs=specs,
        out_specs=[pl.BlockSpec(memory_space=pltpu.VMEM)] * len(outs),
        scratch_shapes=scratch,
        compiler_params=pltpu.CompilerParams(vmem_limit_bytes=20 * 2**20),
        cost_estimate=pl.CostEstimate(flops=flops, bytes_accessed=size, transcendentals=0),
    )(*args)


def contract_last(a, b):
    return lax.dot_general(a, b, (((1,), (1,)), ((), ())), preferred_element_type=F32)


def store_prediction(stack_ref, weights, features, shrink):
    for t in range(features.shape[1] // TILE):
        part = jnp.dot(weights, features[:, t * TILE : (t + 1) * TILE], preferred_element_type=F32)
        stack_ref[t * ROWS : (t + 1) * ROWS] = (part * shrink).astype(BF16).astype(stack_ref.dtype)
    used = features.shape[1] // TILE * ROWS
    if used < stack_ref.shape[0]:
        stack_ref[used:] = jnp.zeros((stack_ref.shape[0] - used, TILE), stack_ref.dtype)


def feature_kernel(img, filt, phase, feat, gram, rows32, patches, taps):
    sides, count = img.shape[:2]
    per = OUT * OUT
    patches[...] = jnp.zeros_like(patches)
    for c in range(OUT):
        for row in range(sides):
            rows32[row * count : (row + 1) * count] = img[row, :, c * PAIR : (c + 1) * PAIR].astype(F32)
        for n in range(count):
            even = rows32[pl.ds(n, OUT, stride=2 * count), :]
            odd = rows32[pl.ds(count + n, OUT, stride=2 * count), :]
            for side in range(2):
                at = c + 1 - side
                if at >= OUT:
                    continue
                first = n * per + at
                patches[2 + side, pl.ds(first, OUT, stride=OUT), :] = even
                patches[4 + side, pl.ds(first, OUT, stride=OUT), :] = odd
                patches[side, pl.ds(first + OUT, OUT - 1, stride=OUT), :] = odd[: OUT - 1]
    windows = jnp.concatenate([patches[k].astype(BF16) for k in range(DEEP // PAIR)], axis=1)
    third = DEEP // 3
    for k in range(3):
        taps[k * third : k * third + CHAN] = jnp.zeros((CHAN, FILT), BF16)
        taps[k * third + CHAN : (k + 1) * third] = filt[k * 3 * CHAN : (k + 1) * 3 * CHAN]
    for block in range(FILT // TILE):
        rows = slice(block * TILE, (block + 1) * TILE)
        response = lax.dot_general(
            taps[:, rows], windows, (((0,), (1,)), ((), ())), preferred_element_type=F32
        )
        turned = jnp.broadcast_to(phase[:, rows], (TILE, TILE)).T
        values = scaled_cosine(response + turned[:, :1])
        live = lax.broadcasted_iota(jnp.int32, values.shape, 1) < count * per
        feat[rows] = jnp.where(live, values, 0.0).astype(BF16)
    at = 0
    for i in range(FILT // TILE):
        for j in range(i + 1):
            gram[at : at + TILE] = contract_last(
                feat[i * TILE : (i + 1) * TILE], feat[j * TILE : (j + 1) * TILE]
            )
            at += TILE


def bit_of(place, level):
    return jnp.bitwise_and(jnp.right_shift(place[0], level), 1)


def halved(place, level, whole, send, keep):
    half = keep.shape[0]
    mine = bit_of(place, level)
    send[...] = whole[pl.ds(pl.multiple_of((1 - mine) * half, 8), half), :].astype(BF16)
    keep[...] = whole[pl.ds(pl.multiple_of(mine * half, 8), half), :]


def first_predict_kernel(shrink, place, weights, feat, send, keep, wide, whole):
    wide[...] = jnp.zeros_like(wide)
    wide[:LABELS] = weights[...]
    store_prediction(whole, wide[...].astype(BF16), feat[...], shrink)
    halved(place, 0, whole, send, keep)


def halving_kernel(level, place, got, kept, send, keep, whole):
    whole[...] = kept[...] + got[...].astype(F32)
    halved(place, level, whole, send, keep)


def summed(ref, parts):
    rows = ref.shape[0] // parts
    total = ref[:rows].astype(F32)
    for k in range(1, parts):
        total += ref[k * rows : (k + 1) * rows].astype(F32)
    return total


def copies(ref, value, parts):
    rows = value.shape[0]
    for k in range(parts):
        ref[k * rows : (k + 1) * rows] = value


def rest(total, first, labels):
    line = lax.broadcasted_iota(jnp.int32, total.shape, 0) + first
    targets = jnp.zeros_like(total)
    for t in range(labels.shape[0]):
        targets += jnp.where(line - t * ROWS == labels[t : t + 1], 1.0, 0.0)
    return (targets - total).astype(BF16)


def residual_kernel(parts, place, got, labels, out):
    out[...] = rest(summed(got, parts), place[0] * out.shape[0], labels)


def first_residual_kernel(levels, place, got, kept, labels, out):
    segment = 0
    for level in range(levels):
        segment = segment * 2 + bit_of(place, level)
    out[...] = rest(kept[...] + got[...].astype(F32), segment * out.shape[0], labels)


def gram_kernel(parts, got, out):
    copies(out, summed(got, parts), parts)


def unstacked(ref, tiles):
    return jnp.concatenate([ref[t * ROWS : (t + 1) * ROWS] for t in range(tiles)], axis=1)


def project_kernel(parts, order, got, feat, out, spread, flat):
    tiles = feat.shape[1] // TILE
    source = got
    if order is not None:
        rows = got.shape[0] // len(order)
        for k, at in enumerate(order):
            flat[at * rows : (at + 1) * rows] = got[k * rows : (k + 1) * rows]
        source = flat
    projected = contract_last(unstacked(source, tiles), feat[...])
    own = ROWS // parts
    rows = spread.shape[0] // parts
    lanes = FILT // TILE
    if own * lanes < rows:
        spread[...] = jnp.zeros_like(spread)
    for k in range(own):
        for t in range(lanes):
            spread[pl.ds(k * lanes + t, parts, stride=rows), :] = projected[
                k * parts : (k + 1) * parts, t * TILE : (t + 1) * TILE
            ]
    out[...] = spread[...].astype(out.dtype)


def two_halves(x):
    high = x.astype(BF16)
    return high, (x - high.astype(F32)).astype(BF16)


def inverse_kernel(ridge, got, matrix, inverse, left, value):
    at = 0
    for i in range(FILT // TILE):
        for j in range(i + 1):
            part = got[at : at + TILE]
            at += TILE
            if i == j:
                eye = lax.broadcasted_iota(jnp.int32, part.shape, 0) == lax.broadcasted_iota(jnp.int32, part.shape, 1)
                part = part + jnp.where(eye, ridge, 0.0)
            else:
                value[j * TILE : (j + 1) * TILE, i * TILE : (i + 1) * TILE] = part.T
            value[i * TILE : (i + 1) * TILE, j * TILE : (j + 1) * TILE] = part
    h = value[...]
    high, rest = two_halves(h)
    matrix[:FILT] = high
    matrix[FILT:] = rest
    left[:, :FILT] = high
    left[:, FILT : 2 * FILT] = high
    left[:, 2 * FILT :] = rest
    largest = jnp.max(jnp.sum(jnp.abs(h), axis=0, keepdims=True))
    scale = 1.0 / largest
    low = 0.98 * ridge * scale
    eye = lax.broadcasted_iota(jnp.int32, h.shape, 0) == lax.broadcasted_iota(jnp.int32, h.shape, 1)
    gain = 4.0 / ((1.0 + low) * (1.0 + low))
    value[...] = gain * scale * (jnp.where(eye, 1.0 + low, 0.0) - scale * h)

    def more(low):
        return low < 1.0 - 1e-4

    def step(low):
        gain = 4.0 / ((1.0 + low) * (1.0 + low))
        x = value[...]
        xh, xl = two_halves(x)
        y = jnp.dot(left[...], jnp.concatenate([xh, xl, xh], axis=0), preferred_element_type=F32)
        yh, yl = two_halves(y)
        xy = jnp.dot(
            jnp.concatenate([xh, xh, xl], axis=1),
            jnp.concatenate([yh, yl, yh], axis=0),
            preferred_element_type=F32,
        )
        value[...] = gain * ((1.0 + low) * x - xy)
        return jnp.minimum(gain * low, 1.0)

    lax.while_loop(more, step, gain * low)
    high, rest = two_halves(value[...])
    inverse[:FILT] = high
    inverse[FILT:] = rest


def times(x, halves):
    rows = x.shape[0]
    both = jnp.concatenate([x.astype(BF16).astype(F32), x - x.astype(BF16).astype(F32)], axis=0).astype(BF16)
    found = jnp.dot(both, halves[:FILT], preferred_element_type=F32) + jnp.dot(
        both, halves[FILT:], preferred_element_type=F32
    )
    return found[:rows] + found[rows:]


def solve_kernel(parts, factor, place, got, weights, matrix, inverse, own_out, out, folded, wide):
    own = ROWS // parts
    lanes = FILT // TILE
    rows = got.shape[0] // parts
    tall = folded.shape[0] // lanes
    folded[...] = jnp.zeros_like(folded)
    folded[:rows] = summed(got, parts)
    projected = jnp.concatenate([folded[pl.ds(t, tall, stride=lanes), :] for t in range(lanes)], axis=1)
    change = times(projected, inverse)
    for _ in range(2):
        change += times(projected - times(change, matrix), inverse)
    if weights.shape[0] == tall:
        now = weights[...]
    else:
        wide[...] = jnp.zeros_like(wide)
        wide[:LABELS] = weights[...]
        held = [wide[pl.ds(place[0] + k * parts, 1), :] for k in range(own)]
        if own < tall:
            held.append(jnp.zeros((tall - own, FILT), F32))
        now = jnp.concatenate(held, axis=0)
    new = now + factor * change
    own_out[...] = new
    for t in range(lanes):
        folded[pl.ds(t, tall, stride=lanes), :] = new[:, t * TILE : (t + 1) * TILE]
    copies(out, folded[:rows].astype(out.dtype), parts)


def predict_kernel(parts, shrink, keep, got, feat, *refs):
    stack = refs[0]
    spread = refs[-1]
    own = ROWS // parts
    rows = got.shape[0] // parts
    lanes = FILT // TILE
    spread[...] = got[...].astype(F32)
    weights = jnp.concatenate(
        [
            jnp.concatenate(
                [spread[pl.ds(k * lanes + t, parts, stride=rows), :] for t in range(lanes)], axis=1
            )
            for k in range(own)
        ],
        axis=0,
    )
    if keep:
        refs[1][...] = weights[:LABELS]
    store_prediction(stack, weights.astype(BF16), feat[...], shrink)


def output_kernel(got, out):
    tiles = -(-out.shape[1] // TILE)
    for t in range(tiles):
        wide = min(TILE, out.shape[1] - t * TILE)
        out[:, t * TILE : t * TILE + wide] = got[t * ROWS : t * ROWS + LABELS, :wide].astype(F32)


def exchange(x, axis):
    parts = lax.axis_size(axis)
    pieces = x.reshape(parts, x.shape[0] // parts, x.shape[1])
    return lax.all_to_all(pieces, axis, 0, 0, tiled=True).reshape(x.shape)


def shards(images, filters, phases, labels, weights):
    groups, blocks = lax.axis_size("img"), lax.axis_size("blk")
    here = labels.shape[0]
    ridge = RIDGE * here * groups
    shrink = 1.0 / math.sqrt(FILT * blocks)
    factor = DAMPING * math.sqrt(FILT * blocks)
    lane_tiles = -(-here // TILE)
    padded = lane_tiles * TILE
    stack_rows = up8(-(-lane_tiles * ROWS // blocks)) * blocks
    fold_rows = up8(ROWS // groups * (FILT // TILE)) * groups
    gram_rows = (FILT // TILE) * (FILT // TILE + 1) // 2 * TILE
    tall = up8(ROWS // groups)

    img_place = lax.axis_index("img").astype(jnp.int32).reshape(1)
    blk_place = lax.axis_index("blk").astype(jnp.int32).reshape(1)
    label_tiles = jnp.pad(labels, (0, padded - here), constant_values=-100000).reshape(lane_tiles, TILE)

    def shape(*dims, dtype=F32):
        return jax.ShapeDtypeStruct(dims, dtype)

    feat, gram_part = call(
        feature_kernel, [shape(FILT, padded, dtype=BF16), shape(gram_rows, TILE)],
        images.transpose(1, 0, 2), filters.T, phases.reshape(1, FILT),
        scratch=[
            pltpu.VMEM((SIDE * images.shape[0], PAIR), F32),
            pltpu.VMEM((DEEP // PAIR, padded, PAIR), F32),
            pltpu.VMEM((DEEP, FILT), BF16),
        ],
        flops=2 * 10**9,
    )
    levels = blocks.bit_length() - 1
    order = [sum((k >> level & 1) << (levels - 1 - level) for level in range(levels)) for k in range(blocks)]

    def halves(level):
        rows = stack_rows >> (level + 1)
        return [shape(rows, TILE, dtype=BF16), shape(rows, TILE)]

    def swapped(send, level):
        pairs = [(k, k ^ (1 << level)) for k in range(blocks)]
        return lax.ppermute(send, "blk", pairs)

    def first_residual():
        send, keep = call(
            lambda *r: first_predict_kernel(shrink, *r), halves(0), blk_place, weights, feat,
            scratch=[pltpu.VMEM((ROWS, FILT), F32), pltpu.VMEM((stack_rows, TILE), F32)],
            flops=10**8,
        )
        for level in range(1, levels):
            send, keep = call(
                lambda *r: halving_kernel(level, *r), halves(level),
                blk_place, swapped(send, level - 1), keep,
                scratch=[pltpu.VMEM((stack_rows >> level, TILE), F32)],
            )
        (mine,) = call(
            lambda *r: first_residual_kernel(levels, *r), [shape(stack_rows // blocks, TILE, dtype=BF16)],
            blk_place, swapped(send, levels - 1), keep, label_tiles,
        )
        return lax.all_gather(mine, "blk", tiled=True)

    def residual_of(stack):
        (mine,) = call(
            lambda *r: residual_kernel(blocks, *r), [shape(stack_rows // blocks, TILE, dtype=BF16)],
            blk_place, exchange(stack, "blk"), label_tiles,
        )
        return lax.all_gather(mine, "blk", tiled=True)

    def projection_of(residual, order):
        (parts,) = call(
            lambda *r: project_kernel(groups, order, *r), [shape(fold_rows, TILE)], residual, feat,
            scratch=[pltpu.VMEM((fold_rows, TILE), F32), pltpu.VMEM((stack_rows, TILE), BF16)],
            flops=10**8,
        )
        return exchange(parts, "img")

    residual = first_residual()
    (gram_sum,) = call(lambda *r: gram_kernel(groups, *r), [shape(gram_rows, TILE)], exchange(gram_part, "img"))
    matrix, inverse = call(
        lambda *r: inverse_kernel(ridge, *r), [shape(2 * FILT, FILT, dtype=BF16)] * 2,
        exchange(gram_sum, "img"),
        scratch=[pltpu.VMEM((FILT, 3 * FILT), BF16), pltpu.VMEM((FILT, FILT), F32)],
        flops=14 * 10**9,
    )
    own = weights
    for step in range(ITERS):
        last = step == ITERS - 1
        projected = projection_of(residual, None if step else order)
        own, spread = call(
            lambda *r: solve_kernel(groups, factor, *r), [shape(tall, FILT), shape(fold_rows, TILE, dtype=BF16)],
            img_place, projected, own, matrix, inverse,
            scratch=[pltpu.VMEM((tall * (FILT // TILE), TILE), F32), pltpu.VMEM((ROWS, FILT), F32)],
            flops=10**8,
        )
        found = call(
            lambda *r: predict_kernel(groups, shrink, last, *r),
            [shape(stack_rows, TILE, dtype=BF16)] + ([shape(LABELS, FILT)] if last else []),
            exchange(spread, "img"), feat,
            scratch=[pltpu.VMEM((fold_rows, TILE), F32)], flops=10**8,
        )
        residual = residual_of(found[0])
    (out,) = call(output_kernel, [shape(LABELS, here)], residual)
    return (found[1], out)


def solution(mesh):
    return jax.shard_map(
        shards,
        mesh=mesh,
        in_specs=(P("img", None, None), P("blk", None), P("blk"), P("img"), P(None, "blk")),
        out_specs=(P(None, "blk"), P(None, "img")),
        check_vma=False,
    )
```

```python
import math

import jax
import jax.numpy as jnp
import numpy as np
from jax import lax
from jax.experimental import pallas as pl
from jax.experimental.pallas import tpu as pltpu
from jax.sharding import PartitionSpec as P

SIDE = 28
CHAN = 64
FILT = 512
LABELS = 150
ITERS = 2
RIDGE = 0.5
DAMPING = 0.75

OUT = SIDE // 2
PAIR = 2 * CHAN
DEEP = 6 * PAIR
ROWS = 160
TILE = 128
BF16 = jnp.bfloat16
F32 = jnp.float32


def cosine_coefficients(degree):
    nodes = np.cos((np.arange(200) + 0.5) * math.pi / 200)
    squares = (nodes + 1) * 0.5 * math.pi**2
    fit = np.polynomial.Chebyshev.fit(
        squares, math.sqrt(2.0) * np.cos(np.sqrt(squares)), degree, domain=[0, math.pi**2]
    )
    return [float(c) for c in fit.convert(kind=np.polynomial.Polynomial).coef]


COS = cosine_coefficients(7)


def scaled_cosine(x):
    turns = jnp.floor(x * (0.5 / math.pi) + 0.5)
    y = (x - turns * 6.28125) - turns * (2 * math.pi - 6.28125)
    u = y * y
    value = u * COS[-1] + COS[-2]
    for c in COS[-3::-1]:
        value = value * u + c
    return value


def up8(n):
    return -(-n // 8) * 8


def call(kernel, outs, *args, scratch=(), name=None, flops=0):
    specs = [
        pl.BlockSpec(memory_space=pltpu.SMEM if a.dtype == jnp.int32 and a.ndim == 1 else pltpu.VMEM)
        for a in args
    ]
    size = sum(math.prod(a.shape) * a.dtype.itemsize for a in (*args, *outs))
    return pl.pallas_call(
        kernel,
        out_shape=outs,
        in_specs=specs,
        out_specs=[pl.BlockSpec(memory_space=pltpu.VMEM)] * len(outs),
        scratch_shapes=scratch,
        compiler_params=pltpu.CompilerParams(vmem_limit_bytes=20 * 2**20),
        name=name,
        cost_estimate=pl.CostEstimate(flops=flops, bytes_accessed=size, transcendentals=0),
    )(*args)


def contract_last(a, b):
    return lax.dot_general(a, b, (((1,), (1,)), ((), ())), preferred_element_type=F32)


def store_prediction(stack_ref, weights, features, shrink):
    for t in range(features.shape[1] // TILE):
        part = jnp.dot(weights, features[:, t * TILE : (t + 1) * TILE], preferred_element_type=F32)
        stack_ref[t * ROWS : (t + 1) * ROWS] = (part * shrink).astype(BF16)
    used = features.shape[1] // TILE * ROWS
    if used < stack_ref.shape[0]:
        stack_ref[used:] = jnp.zeros((stack_ref.shape[0] - used, TILE), BF16)


def feature_kernel(img, filt, phase, feat, gram, rows32, patches, taps):
    sides, count = img.shape[:2]
    per = OUT * OUT
    patches[...] = jnp.zeros_like(patches)
    for c in range(OUT):
        for row in range(sides):
            rows32[row * count : (row + 1) * count] = img[row, :, c * PAIR : (c + 1) * PAIR].astype(F32)
        for n in range(count):
            even = rows32[pl.ds(n, OUT, stride=2 * count), :]
            odd = rows32[pl.ds(count + n, OUT, stride=2 * count), :]
            for side in range(2):
                at = c + 1 - side
                if at >= OUT:
                    continue
                first = n * per + at
                patches[2 + side, pl.ds(first, OUT, stride=OUT), :] = even
                patches[4 + side, pl.ds(first, OUT, stride=OUT), :] = odd
                patches[side, pl.ds(first + OUT, OUT - 1, stride=OUT), :] = odd[: OUT - 1]
    windows = jnp.concatenate([patches[k].astype(BF16) for k in range(DEEP // PAIR)], axis=1)
    third = DEEP // 3
    for k in range(3):
        taps[k * third : k * third + CHAN] = jnp.zeros((CHAN, FILT), BF16)
        taps[k * third + CHAN : (k + 1) * third] = filt[k * 3 * CHAN : (k + 1) * 3 * CHAN]
    for block in range(FILT // TILE):
        rows = slice(block * TILE, (block + 1) * TILE)
        response = lax.dot_general(
            taps[:, rows], windows, (((0,), (1,)), ((), ())), preferred_element_type=F32
        )
        turned = jnp.broadcast_to(phase[:, rows], (TILE, TILE)).T
        values = scaled_cosine(response + turned[:, :1])
        live = lax.broadcasted_iota(jnp.int32, values.shape, 1) < count * per
        feat[rows] = jnp.where(live, values, 0.0).astype(BF16)
    at = 0
    for i in range(FILT // TILE):
        for j in range(i + 1):
            gram[at : at + TILE] = contract_last(
                feat[i * TILE : (i + 1) * TILE], feat[j * TILE : (j + 1) * TILE]
            )
            at += TILE


def first_predict_kernel(shrink, weights, feat, stack, wide):
    wide[...] = jnp.zeros_like(wide)
    wide[:LABELS] = weights[...]
    store_prediction(stack, wide[...].astype(BF16), feat[...], shrink)


def summed(ref, parts):
    rows = ref.shape[0] // parts
    total = ref[:rows].astype(F32)
    for k in range(1, parts):
        total += ref[k * rows : (k + 1) * rows].astype(F32)
    return total


def copies(ref, value, parts):
    rows = value.shape[0]
    for k in range(parts):
        ref[k * rows : (k + 1) * rows] = value


def chip_kernel(place, both, out):
    half = out.shape[0]
    first = pl.multiple_of(jnp.bitwise_and(place[0], 1) * half, 16)
    total = both[pl.ds(first, half), :].astype(F32) + both[pl.ds(first + 2 * half, half), :].astype(F32)
    out[...] = total.astype(BF16)


def residual_kernel(parts, place, got, labels, out):
    total = summed(got, parts)
    segment = jnp.bitwise_and(place[0], 1) * parts + jnp.right_shift(place[0], 1)
    line = lax.broadcasted_iota(jnp.int32, total.shape, 0) + segment * total.shape[0]
    targets = jnp.zeros_like(total)
    for t in range(labels.shape[0]):
        targets += jnp.where(line - t * ROWS == labels[t : t + 1], 1.0, 0.0)
    out[...] = (targets - total).astype(BF16)


def gram_kernel(parts, got, out):
    copies(out, summed(got, parts), parts)


def ordered(got, flat, blocks):
    rows = got.shape[0] // blocks
    for k in range(blocks):
        at = (k % 2) * (blocks // 2) + k // 2
        flat[at * rows : (at + 1) * rows] = got[k * rows : (k + 1) * rows]


def unstacked(ref, tiles):
    return jnp.concatenate([ref[t * ROWS : (t + 1) * ROWS] for t in range(tiles)], axis=1)


def project_kernel(parts, blocks, got, feat, out, spread, flat):
    tiles = feat.shape[1] // TILE
    ordered(got, flat, blocks)
    projected = contract_last(unstacked(flat, tiles), feat[...])
    own = ROWS // parts
    rows = spread.shape[0] // parts
    lanes = FILT // TILE
    if own * lanes < rows:
        spread[...] = jnp.zeros_like(spread)
    for k in range(own):
        for t in range(lanes):
            spread[pl.ds(k * lanes + t, parts, stride=rows), :] = projected[
                k * parts : (k + 1) * parts, t * TILE : (t + 1) * TILE
            ]
    out[...] = spread[...].astype(out.dtype)


def two_halves(x):
    high = x.astype(BF16)
    return high, (x - high.astype(F32)).astype(BF16)


def inverse_kernel(ridge, got, matrix, inverse, left, value):
    at = 0
    for i in range(FILT // TILE):
        for j in range(i + 1):
            part = got[at : at + TILE]
            at += TILE
            if i == j:
                eye = lax.broadcasted_iota(jnp.int32, part.shape, 0) == lax.broadcasted_iota(jnp.int32, part.shape, 1)
                part = part + jnp.where(eye, ridge, 0.0)
            else:
                value[j * TILE : (j + 1) * TILE, i * TILE : (i + 1) * TILE] = part.T
            value[i * TILE : (i + 1) * TILE, j * TILE : (j + 1) * TILE] = part
    h = value[...]
    high, rest = two_halves(h)
    matrix[:FILT] = high
    matrix[FILT:] = rest
    left[:, :FILT] = high
    left[:, FILT : 2 * FILT] = high
    left[:, 2 * FILT :] = rest
    largest = jnp.max(jnp.sum(jnp.abs(h), axis=0, keepdims=True))
    scale = 1.0 / largest
    low = 0.98 * ridge * scale
    eye = lax.broadcasted_iota(jnp.int32, h.shape, 0) == lax.broadcasted_iota(jnp.int32, h.shape, 1)
    gain = 4.0 / ((1.0 + low) * (1.0 + low))
    value[...] = gain * scale * (jnp.where(eye, 1.0 + low, 0.0) - scale * h)

    def more(low):
        return low < 1.0 - 1e-4

    def step(low):
        gain = 4.0 / ((1.0 + low) * (1.0 + low))
        x = value[...]
        xh, xl = two_halves(x)
        y = jnp.dot(left[...], jnp.concatenate([xh, xl, xh], axis=0), preferred_element_type=F32)
        yh, yl = two_halves(y)
        xy = jnp.dot(
            jnp.concatenate([xh, xh, xl], axis=1),
            jnp.concatenate([yh, yl, yh], axis=0),
            preferred_element_type=F32,
        )
        value[...] = gain * ((1.0 + low) * x - xy)
        return jnp.minimum(gain * low, 1.0)

    lax.while_loop(more, step, gain * low)
    high, rest = two_halves(value[...])
    inverse[:FILT] = high
    inverse[FILT:] = rest


def times(x, halves):
    rows = x.shape[0]
    both = jnp.concatenate([x.astype(BF16).astype(F32), x - x.astype(BF16).astype(F32)], axis=0).astype(BF16)
    found = jnp.dot(both, halves[:FILT], preferred_element_type=F32) + jnp.dot(
        both, halves[FILT:], preferred_element_type=F32
    )
    return found[:rows] + found[rows:]


def solve_kernel(parts, factor, place, got, weights, matrix, inverse, own_out, out, folded, wide):
    own = ROWS // parts
    lanes = FILT // TILE
    rows = got.shape[0] // parts
    tall = folded.shape[0] // lanes
    folded[...] = jnp.zeros_like(folded)
    folded[:rows] = summed(got, parts)
    projected = jnp.concatenate([folded[pl.ds(t, tall, stride=lanes), :] for t in range(lanes)], axis=1)
    change = times(projected, inverse)
    for _ in range(2):
        change += times(projected - times(change, matrix), inverse)
    if weights.shape[0] == tall:
        now = weights[...]
    else:
        wide[...] = jnp.zeros_like(wide)
        wide[:LABELS] = weights[...]
        held = [wide[pl.ds(place[0] + k * parts, 1), :] for k in range(own)]
        if own < tall:
            held.append(jnp.zeros((tall - own, FILT), F32))
        now = jnp.concatenate(held, axis=0)
    new = now + factor * change
    own_out[...] = new
    for t in range(lanes):
        folded[pl.ds(t, tall, stride=lanes), :] = new[:, t * TILE : (t + 1) * TILE]
    copies(out, folded[:rows].astype(out.dtype), parts)


def predict_kernel(parts, shrink, keep, got, feat, *refs):
    stack = refs[0]
    spread = refs[-1]
    own = ROWS // parts
    rows = got.shape[0] // parts
    lanes = FILT // TILE
    spread[...] = got[...].astype(F32)
    weights = jnp.concatenate(
        [
            jnp.concatenate(
                [spread[pl.ds(k * lanes + t, parts, stride=rows), :] for t in range(lanes)], axis=1
            )
            for k in range(own)
        ],
        axis=0,
    )
    if keep:
        refs[1][...] = weights[:LABELS]
    store_prediction(stack, weights.astype(BF16), feat[...], shrink)


def output_kernel(blocks, got, out, flat):
    tiles = -(-out.shape[1] // TILE)
    ordered(got, flat, blocks)
    for t in range(tiles):
        wide = min(TILE, out.shape[1] - t * TILE)
        out[:, t * TILE : t * TILE + wide] = flat[t * ROWS : t * ROWS + LABELS, :wide].astype(F32)


def exchange(x, axis):
    parts = lax.axis_size(axis)
    pieces = x.reshape(parts, x.shape[0] // parts, x.shape[1])
    return lax.all_to_all(pieces, axis, 0, 0, tiled=True).reshape(x.shape)


def shards(images, filters, phases, labels, weights):
    groups, blocks = lax.axis_size("img"), lax.axis_size("blk")
    here = labels.shape[0]
    ridge = RIDGE * here * groups
    shrink = 1.0 / math.sqrt(FILT * blocks)
    factor = DAMPING * math.sqrt(FILT * blocks)
    lane_tiles = -(-here // TILE)
    padded = lane_tiles * TILE
    stack_rows = up8(-(-lane_tiles * ROWS // blocks)) * blocks
    fold_rows = up8(ROWS // groups * (FILT // TILE)) * groups
    gram_rows = (FILT // TILE) * (FILT // TILE + 1) // 2 * TILE
    tall = up8(ROWS // groups)

    img_place = lax.axis_index("img").astype(jnp.int32).reshape(1)
    blk_place = lax.axis_index("blk").astype(jnp.int32).reshape(1)
    label_tiles = jnp.pad(labels, (0, padded - here), constant_values=-100000).reshape(lane_tiles, TILE)

    def shape(*dims, dtype=F32):
        return jax.ShapeDtypeStruct(dims, dtype)

    feat, gram_part = call(
        feature_kernel, [shape(FILT, padded, dtype=BF16), shape(gram_rows, TILE)],
        images.transpose(1, 0, 2), filters.T, phases.reshape(1, FILT),
        scratch=[
            pltpu.VMEM((SIDE * images.shape[0], PAIR), F32),
            pltpu.VMEM((DEEP // PAIR, padded, PAIR), F32),
            pltpu.VMEM((DEEP, FILT), BF16),
        ],
        name="features", flops=2 * 10**9,
    )
    (stack,) = call(
        lambda *r: first_predict_kernel(shrink, *r), [shape(stack_rows, TILE, dtype=BF16)], weights, feat,
        scratch=[pltpu.VMEM((ROWS, FILT), F32)], name="predict", flops=10**8,
    )

    def residual_of(stack):
        pairs = [[2 * k, 2 * k + 1] for k in range(blocks // 2)]
        columns = [list(range(core, blocks, 2)) for core in range(2)]
        both = lax.all_gather(stack, "blk", axis_index_groups=pairs, tiled=True)
        (half,) = call(
            chip_kernel, [shape(stack_rows // 2, TILE, dtype=BF16)], blk_place, both, name="chip",
        )
        pieces = half.reshape(blocks // 2, stack_rows // blocks, TILE)
        got = lax.all_to_all(pieces, "blk", 0, 0, tiled=True, axis_index_groups=columns)
        (mine,) = call(
            lambda *r: residual_kernel(blocks // 2, *r), [shape(stack_rows // blocks, TILE, dtype=BF16)],
            blk_place, got.reshape(half.shape), label_tiles, name="residual",
        )
        return lax.all_gather(mine, "blk", tiled=True)

    def projection_of(residual):
        (parts,) = call(
            lambda *r: project_kernel(groups, blocks, *r), [shape(fold_rows, TILE)], residual, feat,
            scratch=[pltpu.VMEM((fold_rows, TILE), F32), pltpu.VMEM((stack_rows, TILE), BF16)],
            name="project", flops=10**8,
        )
        return exchange(parts, "img")

    residual = residual_of(stack)
    (gram_sum,) = call(
        lambda *r: gram_kernel(groups, *r), [shape(gram_rows, TILE)], exchange(gram_part, "img"), name="gram",
    )
    matrix, inverse = call(
        lambda *r: inverse_kernel(ridge, *r), [shape(2 * FILT, FILT, dtype=BF16)] * 2,
        exchange(gram_sum, "img"),
        scratch=[pltpu.VMEM((FILT, 3 * FILT), BF16), pltpu.VMEM((FILT, FILT), F32)],
        name="inverse", flops=14 * 10**9,
    )
    own = weights
    for step in range(ITERS):
        last = step == ITERS - 1
        projected = projection_of(residual)
        own, spread = call(
            lambda *r: solve_kernel(groups, factor, *r), [shape(tall, FILT), shape(fold_rows, TILE, dtype=BF16)],
            img_place, projected, own, matrix, inverse,
            scratch=[pltpu.VMEM((tall * (FILT // TILE), TILE), F32), pltpu.VMEM((ROWS, FILT), F32)],
            name="solve", flops=10**8,
        )
        found = call(
            lambda *r: predict_kernel(groups, shrink, last, *r),
            [shape(stack_rows, TILE, dtype=BF16)] + ([shape(LABELS, FILT)] if last else []),
            exchange(spread, "img"), feat,
            scratch=[pltpu.VMEM((fold_rows, TILE), F32)], name="predict", flops=10**8,
        )
        residual = residual_of(found[0])
    (out,) = call(
        lambda *r: output_kernel(blocks, *r), [shape(LABELS, here)], residual,
        scratch=[pltpu.VMEM((stack_rows, TILE), BF16)], name="output",
    )
    return (found[1], out)


def solution(mesh):
    return jax.shard_map(
        shards,
        mesh=mesh,
        in_specs=(P("img", None, None), P("blk", None), P("blk"), P("img"), P(None, "blk")),
        out_specs=(P(None, "blk"), P(None, "img")),
        check_vma=False,
    )
```
